256 devices in a mesh: sens: 4 (over x_lo, core), src: 64 (over z, x_hi, y).
Axes of the slice: x: 4 (x_hi: 2, x_lo: 2; x = x_hi * 2 + x_lo), y: 4, z: 8, core: 2. Of those that a mesh axis runs over, the one named last changes fastest.
Arguments:
- operator: bfloat16 [128, 2, 512, 8192], P(None, None, 'sens', 'src'), may hold values from -0.75 to 0.75
- right_side: float32 [128, 2, 32, 8192], P('sens', None, None, 'src'), may hold values from -6 to 6
- noise_weights: float32 [128, 512], P('src', 'sens'), may hold values from 0.25 to 4
- damping: float32 [128], P('sens'), may hold values from 1 to 16
Outputs:
- solution: float32 [128, 2, 32, 8192], P('sens', None, None, 'src')
- residual: float32 [128, 2, 32, 8192], P('sens', None, None, 'src')
The draws below stay inside these ranges and needn't reach their ends.
All inputs are finite; a program needn't handle non-finite values.
Results may differ from the reference program's by a relative error of at most 0.025.
Values may be sent and summed in bfloat16 or wider, within the bound.
A program may use at most 128 MiB of HBM per device.

```python
import math
import jax
import jax.numpy as jnp
from jax import lax

FREQS = 128
SENS_DEV = 128
DATASETS = 32
ITERS = 2
SENSORS = 512
SOURCES = 8192
N_SENS = 4


def spiked(values, key, source, target, parts, factor):
    owner, partner = [(jnp.arange(values.shape[dim]) // (values.shape[dim] // parts)).reshape([-1 if axis == dim else 1 for axis in range(values.ndim)]) for dim in (source, target)]
    chosen = jax.random.permutation(key, parts)[partner]
    strong = (owner == chosen) | (owner == (partner + parts // 2) % parts)
    return jnp.where(strong, factor * values, values)


def steps_of(own_key, extent, shards, low, top_value):
    level, own = 1.0, jax.random.fold_in(own_key, 6)
    for dim, shards_of in shards:
        draws = jnp.exp(jax.random.uniform(jax.random.fold_in(own, dim), (shards_of,), jnp.float32, low / len(shards), top_value / len(shards)))
        level = level * jnp.repeat(draws, extent[dim] // shards_of).reshape([-1 if axis == dim else 1 for axis in range(len(extent))])
    return level


def normal_values(own_key, shape, deviation, most, shards=(), dtype=jnp.bfloat16):
    entries = jax.random.normal(own_key, shape, jnp.float32) * deviation
    if len(shards) > 0:
        entries = steps_of(own_key, shape, shards, -0.22, 0.18) * entries
    return jnp.clip(entries, min=-most, max=most).astype(dtype)


def bell_draw_with(key, shape, spread, most, split, heavy, held_as=jnp.bfloat16):
    array = spread * jax.random.normal(key, shape, jnp.float32)
    if split:
        array = array * steps_of(key, shape, split, -0.22, 0.18)
    return jnp.clip(spiked(array, jax.random.fold_in(key, 3), *heavy), -most, most).astype(held_as)


def setup_inputs(seed: int = 0) -> dict:
    splits = jax.random.split(jax.random.key(seed), 5)
    operator = bell_draw_with(splits[0], (FREQS, 2, SENSORS, SOURCES), SENSORS ** -0.5, 0.75, ((2, 4), (3, 64)), (3, 0, 64, 4.0))
    right_side = normal_values(splits[1], (FREQS, 2, DATASETS, SOURCES), 1.0, 6.0, ((0, 4), (3, 64)), jnp.float32)
    noise_weights = jnp.clip(jnp.exp(math.log(4.0) - 2.7725887 * jax.random.uniform(splits[2], (FREQS, SENSORS), jnp.float32) ** steps_of(splits[2], (FREQS, SENSORS), ((0, 64), (1, 4)), -0.2, 0.2)), 0.25, 4.0)
    damping = jnp.clip(jnp.exp(math.log(16.0) - 2.7725887 * jax.random.uniform(splits[3], (FREQS,), jnp.float32) ** steps_of(splits[3], (FREQS,), ((0, 4),), -0.2, 0.2)), 1.0, 16.0)
    return dict(operator=operator, right_side=right_side, noise_weights=noise_weights, damping=damping)


def forward(gmat, vector):
    dims = (((1,), (1,)), ((), ()))

    def multiply(left, right):
        return lax.dot_general(left, right, dims, preferred_element_type=jnp.float32)

    real_part = multiply(vector[0], gmat[0]) - multiply(vector[1], gmat[1])
    imag_part = multiply(vector[1], gmat[0]) + multiply(vector[0], gmat[1])
    return jnp.stack([real_part, imag_part])


def adjoint(gmat, field):
    total = jnp.zeros((2, field.shape[1], gmat.shape[2]), jnp.float32)
    for group in range(N_SENS):
        lower = group * SENS_DEV
        block = gmat[:, lower:lower + SENS_DEV]
        piece = field[:, :, lower:lower + SENS_DEV]
        real_part = jnp.dot(piece[0], block[0], preferred_element_type=jnp.float32) + jnp.dot(piece[1], block[1], preferred_element_type=jnp.float32)
        imag_part = jnp.dot(piece[1], block[0], preferred_element_type=jnp.float32) - jnp.dot(piece[0], block[1], preferred_element_type=jnp.float32)
        partial_sum = lax.optimization_barrier(jnp.stack([real_part, imag_part]).astype(jnp.bfloat16))
        total = total + partial_sum.astype(jnp.float32)
    return total


def hessian(operator, noise_weights, damping, vector):
    rounded = vector.astype(jnp.bfloat16)
    sensor_field = lax.map(lambda pair: forward(pair[0], pair[1]), (operator, rounded))
    weighted = (noise_weights[:, None, None, :] * sensor_field).astype(jnp.bfloat16)
    back = lax.map(lambda pair: adjoint(pair[0], pair[1]), (operator, weighted))
    return back + damping[:, None, None, None] * vector


def reference(operator, right_side, noise_weights, damping):
    solution = jnp.zeros_like(right_side)
    residual = right_side
    direction = right_side
    norm_now = jnp.sum(residual * residual)
    for step in range(ITERS):
        image = hessian(operator, noise_weights, damping, direction)
        alpha = norm_now / jnp.sum(direction * image)
        solution = solution + alpha * direction
        residual = residual - alpha * image
        norm_next = jnp.sum(residual * residual)
        direction = residual + (norm_next / norm_now) * direction
        norm_now = norm_next
    return solution, residual
```

```python
import functools

import jax
import jax.numpy as jnp
from jax import lax
from jax.experimental import pallas as pl
from jax.experimental.pallas import tpu as pltpu
from jax.sharding import PartitionSpec as P

BF16, F32 = jnp.bfloat16, jnp.float32
MESH = pl.DeviceIdType.MESH
NZ, NX, NY, NS = 8, 2, 4, 4
WAVES, ROWS, LANES = 2, 64, 128
OWN = 16
AXES = (("y", "z"), ("z", "y"))
SIZE = {"y": NY, "z": NZ}
STEPS = 8


def flip(value, bit):
    return value + bit - 2 * bit * lax.rem(lax.div(value, bit), 2)


def kernel(
    op_hbm, b_ref, w_ref, d_ref, sol_ref, res_ref,
    op, spectra, part, part2, field0, field1, out, grad, core_in, x_in, xh_out, xh_in,
    image0, image1, w_all, ring_y0, ring_z0, ring_z1, ring_y1, sums, sums_in,
    op_sem, sens_s, sens_r, rs_s, rs_r, ag_s, ag_r, xh_s, xh_r, w_s, w_r, sum_s, sum_r,
):
    s, q = lax.axis_index("sens"), lax.axis_index("src")
    z, xh, y = lax.div(q, 8), lax.rem(lax.div(q, 4), 2), lax.rem(q, 4)
    at = {"y": y, "z": z}
    rings = ((ring_y0, ring_z0), (ring_z1, ring_y1))

    def device(s=s, z=z, xh=xh, y=y):
        return (s, z * 8 + xh * 4 + y)

    def along(axis, step):
        n = SIZE[axis]
        return device(**{axis: lax.rem(at[axis] + n + step, n)})

    core_peer, x_peer, xh_peer = device(s=flip(s, 1)), device(s=flip(s, 2)), device(xh=1 - xh)
    sum_peers = (
        core_peer, x_peer, xh_peer, device(y=flip(y, 1)), device(y=flip(y, 2)),
        device(z=flip(z, 1)), device(z=flip(z, 2)), device(z=flip(z, 4)),
    )
    greeted = (
        core_peer, x_peer, xh_peer, along("y", 1), along("y", -1), device(y=flip(y, 2)),
        along("z", 1), along("z", -1), device(z=flip(z, 2)), device(z=flip(z, 4)),
    )

    def copy_of(src, dst, send_sem, recv_sem, to):
        return pltpu.make_async_remote_copy(
            src_ref=src, dst_ref=dst, send_sem=send_sem, recv_sem=recv_sem,
            device_id=to, device_id_type=MESH,
        )

    def send(*args):
        copy = copy_of(*args)
        copy.start()
        return copy

    load = pltpu.make_async_copy(op_hbm, op, op_sem)
    load.start()
    barrier = pltpu.get_barrier_semaphore()
    for peer in greeted:
        pl.semaphore_signal(barrier, inc=1, device_id=peer, device_id_type=MESH)

    def round_own(wave):
        def step(i, _):
            spectra[wave, s, i] = b_ref[2 * i + wave].astype(BF16)
            return 0
        lax.fori_loop(0, OWN, step, 0)

    for wave in range(WAVES):
        round_own(wave)
    w_all[xh] = jnp.broadcast_to(w_ref[...][:, None, :], (2, 8, LANES))
    pl.semaphore_wait(barrier, len(greeted))
    w_copy = send(w_all.at[xh], w_all.at[xh], w_s, w_r, xh_peer)

    def place(wave, zz, xx, yy):
        return yy * 16 + zz * 2 + xx if wave == 0 else zz * 8 + yy * 2 + xx

    def indices(block, i):
        return 2 * block + lax.div(i, 8), lax.rem(lax.div(i, 4), 2), lax.rem(i, 4)

    def forward(wave, block):
        def step(i, _):
            zz, xx, yy = indices(block, i)
            out_ = lax.dot_general(
                spectra[wave, block, i], op[16 * zz + 8 * xx + 2 * yy + wave],
                (((1,), (1,)), ((), ())), preferred_element_type=F32,
            )
            real = out_[:32, :LANES] - out_[32:, LANES:]
            imag = out_[32:, :LANES] + out_[:32, LANES:]
            part[wave, place(wave, zz, xx, yy)] = jnp.concatenate([real, imag], axis=0).astype(BF16)
            return 0
        lax.fori_loop(0, OWN, step, 0, unroll=4)

    def adjoint(wave, block):
        def step(i, _):
            zz, xx, yy = indices(block, i)
            u = out[wave, place(wave, zz, xx, yy)]
            turned = jnp.concatenate([u[32:], -u[:32]], axis=0)
            f = 16 * zz + 8 * xx + 2 * yy + wave
            g = jnp.dot(u, op[f, :LANES], preferred_element_type=F32)
            g += jnp.dot(turned, op[f, LANES:], preferred_element_type=F32)
            grad[wave, block, i] = g.astype(BF16)
            return 0
        lax.fori_loop(0, OWN, step, 0, unroll=4)

    def sens_forward(wave):
        mine, core, far, both = s, flip(s, 1), flip(s, 2), flip(flip(s, 1), 2)

        def move(k, block, to):
            ref = spectra.at[wave, block]
            return copy_of(ref, ref, sens_s.at[wave, k], sens_r.at[wave, k], to)

        sent = [move(0, mine, x_peer), move(1, mine, core_peer), move(2, far, core_peer)]
        sent[0].start()
        sent[1].start()
        yield
        if wave == 0 and not started:
            load.wait()
            started.append(True)
        forward(wave, mine)
        move(1, core, core_peer).wait_recv()
        forward(wave, core)
        yield
        move(0, far, x_peer).wait_recv()
        sent[2].start()
        forward(wave, far)
        move(2, both, core_peer).wait_recv()
        forward(wave, both)
        for copy in sent:
            copy.wait_send()

    def ring_sum(wave, level, ref, result):
        axis = AXES[wave][level]
        n, me = SIZE[axis], at[axis]
        piece = ref.shape[0] // n
        half, ring = piece // 2, rings[wave][level]
        sent = []

        def span(base, h):
            return pl.ds(base * piece + h * half, half)

        def message(t, h, k):
            d = (1, -1)[k]
            dest = lax.rem(me + n + d * t, n)
            sems = (wave, level, k, t - 1, h)
            return copy_of(
                ref.at[span(dest, h)], ring.at[k, t - 1, pl.ds(h * half, half)],
                rs_s.at[sems], rs_r.at[sems], along(axis, d),
            )

        def go(t, h, k):
            copy = message(t, h, k)
            copy.start()
            sent.append(copy)

        def relay(t, h, k):
            message(t, h, k).wait_recv()
            dest = lax.rem(me + n + (1, -1)[k] * (t - 1), n)

            def add(i, _):
                at_ = dest * piece + h * half + i
                total = ref[at_].astype(F32) + ring[k, t - 1, h * half + i].astype(F32)
                ref[at_] = total.astype(BF16)
                return 0
            lax.fori_loop(0, half, add, 0, unroll=min(half, 2))
            go(t - 1, h, k)

        top = n // 2
        for k in (0, 1):
            go(top, k, k)
        for k in (0, 1):
            go(top - 1, 1 - k, k)
        yield
        for t in range(top, 1, -1):
            for k in (0, 1):
                relay(t, k, k)
            yield
            if t - 1 > 1:
                for k in (0, 1):
                    relay(t - 1, 1 - k, k)
                yield
        for h in (0, 1):
            for k in (0, 1):
                message(1, h, k).wait_recv()

        def last(i, _):
            total = ref[me * piece + i].astype(F32) + ring[0, 0, i].astype(F32)
            result(i, total + ring[1, 0, i].astype(F32))
            return 0
        lax.fori_loop(0, piece, last, 0, unroll=2)
        for copy in sent:
            copy.wait_send()

    def ring_gather(wave, level, ref):
        axis = AXES[wave][level]
        n, me = SIZE[axis], at[axis]
        piece = ref.shape[0] // n
        half = piece // 2
        sent = []

        def message(t, h, k, owner):
            sems = (wave, level, k, t - 1, h)
            where = ref.at[pl.ds(owner * piece + h * half, half)]
            return copy_of(where, where, ag_s.at[sems], ag_r.at[sems], along(axis, (1, -1)[k]))

        def go(t, h, k):
            copy = message(t, h, k, lax.rem(me + n - (1, -1)[k] * (t - 1), n))
            copy.start()
            sent.append(copy)

        def got(t, h, k):
            message(t, h, k, lax.rem(me + n - (1, -1)[k] * t, n)).wait_recv()

        top = n // 2
        for first in (0, 1):
            for k in (0, 1):
                go(1, k if first == 0 else 1 - k, k)
        yield
        for t in range(1, top):
            for k in (0, 1):
                got(t, k, k)
                go(t + 1, k, k)
            yield
            for k in (0, 1):
                got(t, 1 - k, k)
                if t + 1 < top:
                    go(t + 1, 1 - k, k)
            yield
        for k in (0, 1):
            got(top, k, k)
        for copy in sent:
            copy.wait_send()

    def reduce_field(wave, field):
        def keep2(i, total):
            part2[wave, i] = total.astype(BF16)

        def keep1(i, total):
            xh_out[wave, i] = total.astype(BF16)

        yield from ring_sum(wave, 0, part.at[wave], keep2)
        share = part2.at[wave, pl.ds(0, 64 // SIZE[AXES[wave][0]])]
        yield from ring_sum(wave, 1, share, keep1)
        copy = send(xh_out.at[wave], xh_in.at[wave], xh_s.at[wave], xh_r.at[wave], xh_peer)
        yield
        copy.wait_recv()
        field[wave] = xh_out[wave].astype(F32) + xh_in[wave].astype(F32)
        copy.wait_send()

    def spread(wave):
        outer, inner = AXES[wave]
        share = 64 // SIZE[outer]
        own = out.at[wave, pl.ds(at[outer] * share, share)]
        yield from ring_gather(wave, 1, own)
        yield from ring_gather(wave, 0, out.at[wave])

    def own_place(wave):
        return place(wave, z, 0, y)

    def sens_back(wave, image):
        mine, core, far, both = s, flip(s, 1), flip(s, 2), flip(flip(s, 1), 2)

        def to_core(k, block):
            return copy_of(
                grad.at[wave, block], core_in.at[wave, k],
                sens_s.at[wave, 3 + k], sens_r.at[wave, 3 + k], core_peer,
            )

        adjoint(wave, both)
        sent = [to_core(0, both)]
        sent[0].start()
        adjoint(wave, core)
        sent.append(to_core(1, core))
        sent[1].start()
        adjoint(wave, far)
        sent[0].wait_recv()

        def chip(i, _):
            total = grad[wave, far, i].astype(F32) + core_in[wave, 0, i].astype(F32)
            grad[wave, far, i] = total.astype(BF16)
            return 0
        lax.fori_loop(0, OWN, chip, 0, unroll=2)
        sent.append(send(
            grad.at[wave, far], x_in.at[wave], sens_s.at[wave, 5], sens_r.at[wave, 5], x_peer
        ))
        adjoint(wave, mine)
        yield
        sent[1].wait_recv()
        sent[2].wait_recv()

        def whole(i, _):
            total = grad[wave, mine, i].astype(F32) + core_in[wave, 1, i].astype(F32)
            image[2 * i + wave] = total + x_in[wave, i].astype(F32)
            return 0
        lax.fori_loop(0, OWN, whole, 0, unroll=2)
        for copy in sent:
            copy.wait_send()

    def folded(value):
        return jnp.sum(value.reshape(-1, 8, LANES), axis=0)

    def total_of(turn):
        sent = []
        for k in range(STEPS):
            copy = send(
                sums.at[turn, k], sums_in.at[turn, k], sum_s.at[turn, k], sum_r.at[turn, k],
                sum_peers[k],
            )
            sent.append(copy)
            yield
            copy.wait_recv()
            sums[turn, k + 1] = sums[turn, k] + sums_in[turn, k]
        for copy in sent:
            copy.wait_send()

    def scalar(turn, k):
        return jnp.sum(sums[turn, STEPS, k], keepdims=True)

    started = []
    tasks = {}
    zero = jnp.zeros((8, LANES), F32)

    def drain(name):
        for _ in tasks.get(name, ()):
            pass

    def weigh(wave, field):
        curve = zero
        for k in range(2):
            w = w_all[k, wave, 0:1]
            u = w * field[wave, k]
            out[wave, own_place(wave) + k] = u.astype(BF16)
            curve += 0.5 * folded(u * field[wave, k])
        return curve

    sums[0, 0] = jnp.zeros((2, 8, LANES), F32)
    sums[1, 0] = jnp.zeros((2, 8, LANES), F32)
    sums[2, 0] = jnp.zeros((2, 8, LANES), F32)

    def first_norms():
        def step(i, carry):
            square = folded(b_ref[i] * b_ref[i])
            return carry[0] + square, carry[1] + d_ref[i] * square
        rr, bdb = lax.fori_loop(0, 2 * OWN, step, (zero, zero))
        sums[0, 0, 0] = rr
        sums[0, 0, 1] += bdb

    def run(wave):
        yield from sens_forward(wave)
        yield from reduce_field(wave, field0)
        if wave == 0:
            w_copy.wait()
        sums[0, 0, 1] += weigh(wave, field0)
        yield "weighed"
        yield from spread(wave)
        yield from sens_back(wave, image0)

        def step(i, _):
            at_ = 2 * i + wave
            image = image0[at_] + d_ref[at_] * b_ref[at_]
            image0[at_] = image
            spectra[wave, s, i] = image.astype(BF16)
            return 0
        lax.fori_loop(0, OWN, step, 0, unroll=2)
        yield "image"
        yield from sens_forward(wave)
        yield from reduce_field(wave, field1)
        yield "field"
        drain("second")
        alpha, beta = coefficients()
        for k in range(2):
            field1[wave, k] = (1.0 + beta) * field0[wave, k] - alpha * field1[wave, k]
        sums[2, 0, 0] += weigh(wave, field1)
        yield "weighed"
        yield from spread(wave)
        yield from sens_back(wave, image1)

    def coefficients():
        rr0 = scalar(0, 0)
        return rr0 / scalar(0, 1), scalar(1, 0) / rr0

    def second_norm():
        drain("first")
        alpha = scalar(0, 0) / scalar(0, 1)

        def step(i, carry):
            residual = b_ref[i] - alpha * image0[i]
            return carry + folded(residual * residual)
        sums[1, 0, 0] = lax.fori_loop(0, 2 * OWN, step, zero)

    def third_norm():
        alpha, beta = coefficients()

        def step(i, carry):
            p = (1.0 + beta) * b_ref[i] - alpha * image0[i]
            return carry + d_ref[i] * folded(p * p)
        sums[2, 0, 0] += lax.fori_loop(0, 2 * OWN, step, zero)

    waves = [run(0), run(1)]
    seen = []
    alive = [True, True]
    first = True
    while any(alive):
        for wave in range(WAVES):
            if not alive[wave]:
                continue
            try:
                mark = next(waves[wave])
            except StopIteration:
                alive[wave] = False
                continue
            if mark:
                seen.append(mark)
                if mark == "weighed" and seen.count(mark) == 2:
                    tasks["first"] = total_of(0)
                if mark == "image" and seen.count(mark) == 2:
                    second_norm()
                    tasks["second"] = total_of(1)
                if mark == "weighed" and seen.count(mark) == 4:
                    third_norm()
                    tasks["third"] = total_of(2)
        if first:
            first_norms()
            first = False
        for task in tasks.values():
            next(task, None)

    drain("third")
    alpha, beta = coefficients()
    alpha1 = scalar(1, 0) / scalar(2, 0)

    def finish(i, _):
        residual = b_ref[i] - alpha * image0[i]
        p = residual + beta * b_ref[i]
        sol_ref[i] = alpha * b_ref[i] + alpha1 * p
        res_ref[i] = residual - alpha1 * (image1[i] + d_ref[i] * p)
        return 0
    lax.fori_loop(0, 2 * OWN, finish, 0, unroll=2)


def body(operator, right_side, noise_weights, damping):
    shape = right_side.shape
    op = operator.reshape(128, 256, LANES)
    b = right_side.reshape(2 * OWN, ROWS, LANES)
    block = (ROWS, LANES)
    vmem = pl.BlockSpec(memory_space=pltpu.VMEM)
    dma = pltpu.SemaphoreType.DMA
    scratch = [
        pltpu.VMEM((128, 256, LANES), BF16),
        pltpu.VMEM((WAVES, NS, OWN, *block), BF16),
        pltpu.VMEM((WAVES, 64, *block), BF16),
        pltpu.VMEM((WAVES, 16, *block), BF16),
        pltpu.VMEM((WAVES, 2, *block), F32),
        pltpu.VMEM((WAVES, 2, *block), F32),
        pltpu.VMEM((WAVES, 64, *block), BF16),
        pltpu.VMEM((WAVES, NS, OWN, *block), BF16),
        pltpu.VMEM((WAVES, 2, OWN, *block), BF16),
        pltpu.VMEM((WAVES, OWN, *block), BF16),
        pltpu.VMEM((WAVES, 2, *block), BF16),
        pltpu.VMEM((WAVES, 2, *block), BF16),
        pltpu.VMEM((2 * OWN, *block), F32),
        pltpu.VMEM((2 * OWN, *block), F32),
        pltpu.VMEM((2, 2, 8, LANES), F32),
        pltpu.VMEM((2, 2, 16, *block), BF16),
        pltpu.VMEM((2, 4, 2, *block), BF16),
        pltpu.VMEM((2, 4, 8, *block), BF16),
        pltpu.VMEM((2, 2, 2, *block), BF16),
        pltpu.VMEM((3, STEPS + 1, 2, 8, LANES), F32),
        pltpu.VMEM((3, STEPS, 2, 8, LANES), F32),
        dma, dma((WAVES, 6)), dma((WAVES, 6)),
        dma((WAVES, 2, 2, 4, 2)), dma((WAVES, 2, 2, 4, 2)),
        dma((WAVES, 2, 2, 4, 2)), dma((WAVES, 2, 2, 4, 2)),
        dma((WAVES,)), dma((WAVES,)), dma, dma, dma((3, STEPS)), dma((3, STEPS)),
    ]
    result = jax.ShapeDtypeStruct(b.shape, F32)
    sol, res = pl.pallas_call(
        kernel,
        out_shape=(result, result),
        in_specs=[
            pl.BlockSpec(memory_space=pl.ANY), vmem, vmem,
            pl.BlockSpec(memory_space=pltpu.SMEM),
        ],
        out_specs=(vmem, vmem),
        scratch_shapes=scratch,
        compiler_params=pltpu.CompilerParams(
            collective_id=0, has_side_effects=True, vmem_limit_bytes=56 * 2**20
        ),
        name="solve",
    )(op, b, noise_weights, damping)
    return sol.reshape(shape), res.reshape(shape)


def solution(mesh):
    sides = P("sens", None, None, "src")
    return jax.shard_map(
        body,
        mesh=mesh,
        in_specs=(P(None, None, "sens", "src"), sides, P("src", "sens"), P("sens")),
        out_specs=(sides, sides),
        check_vma=False,
    )
```

```python
import functools

import jax
import jax.numpy as jnp
from jax import lax
from jax.experimental import pallas as pl
from jax.experimental.pallas import tpu as pltpu
from jax.sharding import PartitionSpec as P

BF16, F32 = jnp.bfloat16, jnp.float32
MESH = pl.DeviceIdType.MESH
NZ, NX, NY, NS = 8, 2, 4, 4
LIMIT = 51
SPLIT = 2
WAVES, ROWS, LANES = 2 * SPLIT, 64 // SPLIT, 128
HALF = ROWS // 2
OWN = 16
AXES = (("y", "z"), ("z", "y")) * SPLIT
SIZE = {"y": NY, "z": NZ}
MESSAGES, LAST = 13, 5


def flip(value, bit):
    return value + bit - 2 * bit * lax.rem(lax.div(value, bit), 2)


RATE = {"x": 46.0e3, "y": 46.0e3, "z": 46.0e3, "core": 250.0e3, "xh": 46.0e3}
DELAY = {"x": 1.7, "y": 1.7, "z": 1.7, "core": 0.9, "xh": 2.5}
BLOCK = ROWS * LANES * 2


class Plan:
    def __init__(self):
        self.now, self.free, self.done = 0.0, {}, {}

    def spend(self, time):
        self.now += time

    def sent(self, link, way, size):
        begin = max(self.now, self.free.get((link, way), 0.0))
        self.free[link, way] = begin + size / RATE.get(link, 46.0e3)
        return self.free[link, way] + DELAY[link]

    def due(self, mark):
        return self.done.get(mark, float("inf")) if isinstance(mark, str) else mark

    def run(self, tasks):
        waiting = [[task, 0.0] for task in tasks]
        while waiting:
            entry = min(waiting, key=lambda pair: self.due(pair[1]))
            self.now = max(self.now, self.due(entry[1]))
            assert self.now < float("inf")
            value = next(entry[0], None)
            if value is None:
                waiting.remove(entry)
            elif isinstance(value, (str, float)):
                entry[1] = value
            else:
                waiting.append([value, 0.0])


def kernel(
    op_hbm, b_hbm, w_ref, d_ref, image0, image1, scalars,
    op, b_ref, spectra, part, part2, field0, field1, out, grad, core_in, x_in, xh_out, xh_in,
    w_all, ring_ya, ring_zb, ring_za, ring_yb, sums, sums_in,
    op_sem, b_sem, sens_s, sens_r, rs_s, rs_r, ag_s, ag_r, xh_s, xh_r, w_s, w_r, sum_s, sum_r,
):
    plan = Plan()
    s, q = lax.axis_index("sens"), lax.axis_index("src")
    z, xh, y = lax.div(q, 8), lax.rem(lax.div(q, 4), 2), lax.rem(q, 4)
    at = {"y": y, "z": z}
    rings = ((ring_ya, ring_zb), (ring_za, ring_yb))

    def device(s=s, z=z, xh=xh, y=y):
        return (s, z * 8 + xh * 4 + y)

    def along(axis, step):
        n = SIZE[axis]
        return device(**{axis: lax.rem(at[axis] + n + step, n)})

    core_peer, x_peer, xh_peer = device(s=flip(s, 1)), device(s=flip(s, 2)), device(xh=1 - xh)
    greeted = (
        core_peer, x_peer, xh_peer, along("y", 1), along("y", -1), along("z", 1), along("z", -1),
    )

    def copy_of(src, dst, send_sem, recv_sem, to):
        return pltpu.make_async_remote_copy(
            src_ref=src, dst_ref=dst, send_sem=send_sem, recv_sem=recv_sem,
            device_id=to, device_id_type=MESH,
        )

    unsettled = {}

    def begin(name, copy, link, way, size):
        copy.start()
        unsettled.setdefault(name, []).append(copy)
        return plan.sent(link, way, size)

    def settle(name):
        for copy in unsettled.pop(name, ()):
            copy.wait_send()

    b_load = pltpu.make_async_copy(b_hbm, b_ref, b_sem)
    b_load.start()
    load = pltpu.make_async_copy(op_hbm, op, op_sem)
    load.start()
    barrier = pltpu.get_barrier_semaphore()
    for peer in greeted:
        pl.semaphore_signal(barrier, inc=1, device_id=peer, device_id_type=MESH)

    def rows(ref, i, wave):
        low = HALF * (wave // 2)
        parts = [ref[i, pl.ds(low, HALF)], ref[i, pl.ds(32 + low, HALF)]]
        return jnp.concatenate(parts, axis=0)

    def round_own(wave):
        def step(i, _):
            spectra[wave, s, i] = rows(b_ref, 2 * i + wave % 2, wave).astype(BF16)
            return 0
        lax.fori_loop(0, OWN, step, 0)

    b_load.wait()
    for wave in range(WAVES):
        round_own(wave)
    w_all[xh] = jnp.broadcast_to(w_ref[...][:, None, :], (2, 8, LANES))
    pl.semaphore_wait(barrier, len(greeted))

    def place(wave, zz, xx, yy):
        return yy * 16 + zz * 2 + xx if wave % 2 == 0 else zz * 8 + yy * 2 + xx

    def indices(block, i):
        return 2 * block + lax.div(i, 8), lax.rem(lax.div(i, 4), 2), lax.rem(i, 4)

    def forward(wave, one, two):
        def step(j, _):
            block, i = one + (two - one) * lax.div(j, OWN), lax.rem(j, OWN)
            zz, xx, yy = indices(block, i)
            out_ = lax.dot_general(
                spectra[wave, block, i], op[16 * zz + 8 * xx + 2 * yy + wave % 2],
                (((1,), (1,)), ((), ())), preferred_element_type=F32,
            )
            real = out_[:HALF, :LANES] - out_[HALF:, LANES:]
            imag = out_[HALF:, :LANES] + out_[:HALF, LANES:]
            part[wave, place(wave, zz, xx, yy)] = jnp.concatenate([real, imag], axis=0).astype(BF16)
            return 0
        lax.fori_loop(0, 2 * OWN, step, 0, unroll=16)
        plan.spend(1.4 / SPLIT + 0.2)

    def adjoint(wave, one, two):
        def step(j, _):
            block, i = one + (two - one) * lax.div(j, OWN), lax.rem(j, OWN)
            zz, xx, yy = indices(block, i)
            u = out[wave, place(wave, zz, xx, yy)]
            turned = jnp.concatenate([u[HALF:], -u[:HALF]], axis=0)
            f = 16 * zz + 8 * xx + 2 * yy + wave % 2
            g = jnp.dot(u, op[f, :LANES], preferred_element_type=F32)
            g += jnp.dot(turned, op[f, LANES:], preferred_element_type=F32)
            grad[wave, block, i] = g.astype(BF16)
            return 0
        lax.fori_loop(0, 2 * OWN, step, 0, unroll=16)
        plan.spend(1.4 / SPLIT + 0.2)

    def sens_begin(wave):
        mine, far = s, flip(s, 2)

        def move(k, block, to):
            ref = spectra.at[wave, block]
            return copy_of(ref, ref, sens_s.at[wave, k], sens_r.at[wave, k], to)

        size, name = OWN * BLOCK, ("spectra", wave)
        eta_x = begin(name, move(0, mine, x_peer), "x", 1, size)
        eta_core = begin(name, move(1, mine, core_peer), "core", 1, size)
        return eta_x, eta_core, move

    def sens_forward(wave, begun):
        mine, core, far, both = s, flip(s, 1), flip(s, 2), flip(flip(s, 1), 2)
        eta_x, eta_core, move = begun
        settle(("part", wave))
        settle(("out", wave))
        if not loaded:
            load.wait()
            loaded.append(True)
        yield eta_core
        move(1, core, core_peer).wait_recv()
        forward(wave, mine, core)
        yield eta_x
        move(0, far, x_peer).wait_recv()
        yield begin(("spectra", wave), move(2, far, core_peer), "core", 1, OWN * BLOCK)
        move(2, both, core_peer).wait_recv()
        forward(wave, far, both)

    def ring_sum(wave, level, ref, result, name):
        axis = AXES[wave][level]
        n, me = SIZE[axis], at[axis]
        piece = ref.shape[0] // n
        half, ring = piece // 2, rings[wave % 2][level].at[wave // 2]
        eta = {}

        top = n // 2

        def span(h):
            return (0, piece) if h is None else (h * half, half)

        def message(t, h, k):
            d = (1, -1)[k]
            dest = lax.rem(me + n + d * t, n)
            low, size = span(h)
            sems = (wave, level, k, t - 1, h or 0)
            return copy_of(
                ref.at[pl.ds(dest * piece + low, size)], ring.at[k, t - 1, pl.ds(low, size)],
                rs_s.at[sems], rs_r.at[sems], along(axis, d),
            )

        def go(t, h, k):
            eta[t, h, k] = begin(name, message(t, h, k), axis, k, span(h)[1] * BLOCK)

        def add(t, h, k):
            message(t, h, k).wait_recv()
            dest = lax.rem(me + n + (1, -1)[k] * (t - 1), n)
            low, size = span(h)

            def step(i, _):
                at_ = dest * piece + low + i
                total = ref[at_].astype(F32) + ring[k, t - 1, low + i].astype(F32)
                ref[at_] = total.astype(BF16)
                return 0
            lax.fori_loop(0, size, step, 0, unroll=min(size, 2))
            plan.spend(0.1 + 0.01 * size / SPLIT)

        for k in (0, 1):
            go(top, k, k)
        if level == 0:
            for k in (0, 1):
                go(top - 1, 1 - k, k)
        for t in range(top, 1, -1):
            whole = level == 1
            for k in (0, 1):
                h = k if t == top or not whole else None
                yield eta[t, h, k]
                add(t, h, k)
                go(t - 1, None if whole else k, k)
            if t - 1 > 1 and not whole:
                for k in (0, 1):
                    yield eta[t - 1, 1 - k, k]
                    add(t - 1, 1 - k, k)
                    go(t - 2, 1 - k, k)
        final = [(1, h, k) for h in ((None,) if level == 1 else (0, 1)) for k in (0, 1)]
        yield max(eta[key] for key in final)
        for key in final:
            message(*key).wait_recv()

        def last(i, _):
            total = ref[me * piece + i].astype(F32) + ring[0, 0, i].astype(F32)
            result(i, total + ring[1, 0, i].astype(F32))
            return 0
        lax.fori_loop(0, piece, last, 0, unroll=2)
        plan.spend(0.1 + 0.015 * piece / SPLIT)

    def ring_gather(wave, level, ref):
        axis = AXES[wave][level]
        n, me = SIZE[axis], at[axis]
        piece = ref.shape[0] // n
        half = piece // 2
        eta = {}
        top = n // 2

        def message(t, h, k, owner):
            low, size = (0, piece) if h is None else (h * half, half)
            sems = (wave, level, k, t - 1, h or 0)
            where = ref.at[pl.ds(owner * piece + low, size)]
            return copy_of(where, where, ag_s.at[sems], ag_r.at[sems], along(axis, (1, -1)[k]))

        def go(t, h, k):
            copy = message(t, h, k, lax.rem(me + n - (1, -1)[k] * (t - 1), n))
            size = (piece if h is None else half) * BLOCK
            eta[t, h, k] = begin(("out", wave), copy, axis, k, size)

        def got(t, h, k):
            message(t, h, k, lax.rem(me + n - (1, -1)[k] * t, n)).wait_recv()

        if level == 1:
            for k in (0, 1):
                go(1, None, k)
            for t in range(1, top):
                for k in (0, 1):
                    yield eta[t, None, k]
                    got(t, None, k)
                    go(t + 1, None if t + 1 < top else k, k)
        else:
            for first in (0, 1):
                for k in (0, 1):
                    go(1, k if first == 0 else 1 - k, k)
            for t in range(1, top):
                for k in (0, 1):
                    yield eta[t, k, k]
                    got(t, k, k)
                    go(t + 1, k, k)
                for k in (0, 1):
                    if t + 1 < top:
                        yield eta[t, 1 - k, k]
                        got(t, 1 - k, k)
                        go(t + 1, 1 - k, k)
        yield max(eta[top, k, k] for k in (0, 1))
        if level == 0:
            for k in (0, 1):
                got(top - 1, 1 - k, k)
        for k in (0, 1):
            got(top, k, k)

    def reduce_field(wave, field):
        def keep2(i, total):
            part2[wave, i] = total.astype(BF16)

        def keep1(i, total):
            xh_out[wave, i] = total.astype(BF16)

        settle(("part2", wave))
        settle(("xh", wave))
        yield from ring_sum(wave, 0, part.at[wave], keep2, ("part", wave))
        share = part2.at[wave, pl.ds(0, 64 // SIZE[AXES[wave][0]])]
        yield from ring_sum(wave, 1, share, keep1, ("part2", wave))
        copy = copy_of(xh_out.at[wave], xh_in.at[wave], xh_s.at[wave], xh_r.at[wave], xh_peer)
        yield begin(("xh", wave), copy, "xh", 1, 2 * BLOCK)
        copy.wait_recv()
        field[wave] = xh_out[wave].astype(F32) + xh_in[wave].astype(F32)

    def spread(wave):
        outer = AXES[wave][0]
        share = 64 // SIZE[outer]
        own = out.at[wave, pl.ds(at[outer] * share, share)]
        yield from ring_gather(wave, 1, own)
        yield from ring_gather(wave, 0, out.at[wave])

    def sens_back(wave, image):
        mine, core, far, both = s, flip(s, 1), flip(s, 2), flip(flip(s, 1), 2)
        name, size = ("grad", wave), OWN * BLOCK

        def to_core(k, block):
            return copy_of(
                grad.at[wave, block], core_in.at[wave, k],
                sens_s.at[wave, 3 + k], sens_r.at[wave, 3 + k], core_peer,
            )

        settle(name)
        settle(("spectra", wave))
        adjoint(wave, both, far)
        first = to_core(0, both)
        eta = begin(name, first, "core", 1, size)
        yield eta
        first.wait_recv()

        def chip(i, _):
            total = grad[wave, far, i].astype(F32) + core_in[wave, 0, i].astype(F32)
            grad[wave, far, i] = total.astype(BF16)
            return 0
        lax.fori_loop(0, OWN, chip, 0, unroll=2)
        plan.spend(0.1 + 0.2 / SPLIT)
        across = copy_of(
            grad.at[wave, far], x_in.at[wave], sens_s.at[wave, 5], sens_r.at[wave, 5], x_peer
        )
        eta = begin(name, across, "x", 1, size)
        adjoint(wave, core, mine)
        second = to_core(1, core)
        begin(name, second, "core", 1, size)
        yield eta
        second.wait_recv()
        across.wait_recv()

        def whole(i, _):
            total = grad[wave, mine, i].astype(F32) + core_in[wave, 1, i].astype(F32)
            total += x_in[wave, i].astype(F32)
            at_ = 2 * i + wave % 2
            if image is image0:
                total += d_ref[at_] * rows(b_ref, at_, wave)
                spectra[wave, s, i] = total.astype(BF16)
            low = HALF * (wave // 2)
            image[at_, pl.ds(low, HALF)] = total[:HALF]
            image[at_, pl.ds(32 + low, HALF)] = total[HALF:]
            return 0
        lax.fori_loop(0, OWN, whole, 0, unroll=2)
        plan.spend(0.1 + 0.3 / SPLIT)

    def folded(value):
        return jnp.sum(value.reshape(-1, 8, LANES), axis=0)

    def total_of(turn):
        def message(m, source, to):
            return copy_of(
                source, sums_in.at[turn, m], sum_s.at[turn, m], sum_r.at[turn, m], to
            )

        for m, (link, peer) in enumerate((("core", core_peer), ("x", x_peer), ("xh", xh_peer))):
            copy = message(m, sums.at[turn, m], peer)
            yield begin("sums", copy, link, 1, 8192)
            copy.wait_recv()
            sums[turn, m + 1] = sums[turn, m] + sums_in[turn, m]
        m, level = 3, 3
        for axis in ("y", "z"):
            top = SIZE[axis] // 2
            total = sums[turn, level]
            last = [sums.at[turn, level]] * 2
            for t in range(1, top + 1):
                ways = (0, 1) if t < top else (0,)
                copies = []
                for k in ways:
                    copy = message(m, last[k], along(axis, (1, -1)[k]))
                    eta = begin("sums", copy, axis, k, 8192)
                    copies.append(copy)
                    last[k] = sums_in.at[turn, m]
                    m += 1
                yield eta
                for k in ways:
                    copies[k].wait_recv()
                    total = total + last[k][...]
            level += 1
            sums[turn, level] = total
        plan.done["total%d" % turn] = plan.now

    def scalar(turn, k):
        return jnp.sum(sums[turn, LAST, k], keepdims=True)

    loaded = []
    counts = {}
    zero = jnp.zeros((8, LANES), F32)

    def arrived(name):
        counts[name] = counts.get(name, 0) + 1
        if counts[name] == WAVES:
            plan.done[name] = plan.now

    def weigh(wave, field):
        curve = zero
        for k in range(2):
            w = w_all[k, wave % 2, 0:1]
            u = w * field[wave, k]
            out[wave, place(wave, z, 0, y) + k] = u.astype(BF16)
            curve += 0.5 * folded(u * field[wave, k])
        plan.spend(0.1 + 0.2 / SPLIT)
        return curve

    def coefficients():
        rr0 = scalar(0, 0)
        return rr0 / scalar(0, 1), scalar(1, 0) / rr0

    def run(wave):
        yield from sens_forward(wave, begun[wave])
        yield from reduce_field(wave, field0)
        if "w" not in counts:
            w_copy.wait_recv()
            counts["w"] = 1
        sums[0, 0, 1] += weigh(wave, field0)
        arrived("weighed0")
        yield from spread(wave)
        yield from sens_back(wave, image0)
        now = sens_begin(wave)
        arrived("image")
        yield from sens_forward(wave, now)
        yield from reduce_field(wave, field1)
        yield "total1"
        alpha, beta = coefficients()
        for k in range(2):
            field1[wave, k] = (1.0 + beta) * field0[wave, k] - alpha * field1[wave, k]
        sums[2, 0, 0] += weigh(wave, field1)
        arrived("weighed1")
        yield from spread(wave)
        yield from sens_back(wave, image1)

    def norms():
        yield "weighed0"
        yield from total_of(0)
        yield "image"
        alpha = scalar(0, 0) / scalar(0, 1)

        def second(i, carry):
            residual = b_ref[i] - alpha * image0[i]
            return carry + folded(residual * residual)
        sums[1, 0, 0] = lax.fori_loop(0, 2 * OWN, second, zero)
        plan.spend(1.0)
        yield from total_of(1)
        yield "weighed1"
        alpha, beta = coefficients()

        def third(i, carry):
            p = (1.0 + beta) * b_ref[i] - alpha * image0[i]
            return carry + d_ref[i] * folded(p * p)
        sums[2, 0, 0] += lax.fori_loop(0, 2 * OWN, third, zero)
        plan.spend(1.0)
        yield from total_of(2)

    begun = [sens_begin(wave) for wave in range(WAVES)]
    w_copy = copy_of(w_all.at[xh], w_all.at[xh], w_s, w_r, xh_peer)
    begin("w", w_copy, "xh", 1, 8192)
    for turn in range(3):
        sums[turn, 0] = jnp.zeros((2, 8, LANES), F32)

    def first_norms(i, carry):
        square = folded(b_ref[i] * b_ref[i])
        return carry[0] + square, carry[1] + d_ref[i] * square
    rr, bdb = lax.fori_loop(0, 2 * OWN, first_norms, (zero, zero))
    sums[0, 0, 0] = rr
    sums[0, 0, 1] = bdb
    plan.spend(1.0)

    plan.run([*map(run, range(WAVES)), norms()])
    alpha, beta = coefficients()
    alpha1 = scalar(1, 0) / scalar(2, 0)
    for k, value in enumerate((alpha, beta, alpha1)):
        scalars[k] = jnp.broadcast_to(value, (8, LANES))
    for name in list(unsettled):
        settle(name)


def body(operator, right_side, noise_weights, damping):
    shape = right_side.shape
    op = operator.reshape(128, 256, LANES)
    b = right_side.reshape(2 * OWN, 2 * 32, LANES)
    block = (ROWS, LANES)
    vmem = pl.BlockSpec(memory_space=pltpu.VMEM)
    dma = pltpu.SemaphoreType.DMA
    scratch = [
        pltpu.VMEM((128, 256, LANES), BF16),
        pltpu.VMEM((2 * OWN, 2 * 32, LANES), F32),
        pltpu.VMEM((WAVES, NS, OWN, *block), BF16),
        pltpu.VMEM((WAVES, 64, *block), BF16),
        pltpu.VMEM((WAVES, 16, *block), BF16),
        pltpu.VMEM((WAVES, 2, *block), F32),
        pltpu.VMEM((WAVES, 2, *block), F32),
        pltpu.VMEM((WAVES, 64, *block), BF16),
        pltpu.VMEM((WAVES, NS, OWN, *block), BF16),
        pltpu.VMEM((WAVES, 2, OWN, *block), BF16),
        pltpu.VMEM((WAVES, OWN, *block), BF16),
        pltpu.VMEM((WAVES, 2, *block), BF16),
        pltpu.VMEM((WAVES, 2, *block), BF16),
        pltpu.VMEM((2, 2, 8, LANES), F32),
        pltpu.VMEM((SPLIT, 2, 2, 16, *block), BF16),
        pltpu.VMEM((SPLIT, 2, 4, 2, *block), BF16),
        pltpu.VMEM((SPLIT, 2, 4, 8, *block), BF16),
        pltpu.VMEM((SPLIT, 2, 2, 2, *block), BF16),
        pltpu.VMEM((3, LAST + 1, 2, 8, LANES), F32),
        pltpu.VMEM((3, MESSAGES, 2, 8, LANES), F32),
        dma, dma, dma((WAVES, 6)), dma((WAVES, 6)),
        dma((WAVES, 2, 2, 4, 2)), dma((WAVES, 2, 2, 4, 2)),
        dma((WAVES, 2, 2, 4, 2)), dma((WAVES, 2, 2, 4, 2)),
        dma((WAVES,)), dma((WAVES,)), dma, dma, dma((3, MESSAGES)), dma((3, MESSAGES)),
    ]
    result = jax.ShapeDtypeStruct(b.shape, F32)
    image0, image1, scalars = pl.pallas_call(
        kernel,
        out_shape=(result, result, jax.ShapeDtypeStruct((3, 8, LANES), F32)),
        in_specs=[
            pl.BlockSpec(memory_space=pltpu.HBM), pl.BlockSpec(memory_space=pltpu.HBM), vmem,
            pl.BlockSpec(memory_space=pltpu.SMEM),
        ],
        out_specs=(vmem, vmem, vmem),
        scratch_shapes=scratch,
        compiler_params=pltpu.CompilerParams(
            collective_id=0, has_side_effects=True, vmem_limit_bytes=LIMIT * 2**20
        ),
        name="solve",
    )(op, b, noise_weights, damping)
    alpha, beta, alpha1 = (scalars[k : k + 1, 0:1] for k in range(3))
    d = damping[:, None, None]
    residual = b - alpha * image0
    direction = residual + beta * b
    sol = alpha * b + alpha1 * direction
    res = residual - alpha1 * (image1 + d * direction)
    return sol.reshape(shape), res.reshape(shape)


def solution(mesh):
    sides = P("sens", None, None, "src")
    return jax.shard_map(
        body,
        mesh=mesh,
        in_specs=(P(None, None, "sens", "src"), sides, P("src", "sens"), P("sens")),
        out_specs=(sides, sides),
        check_vma=False,
    )
```

```python
import functools

import jax
import jax.numpy as jnp
from jax import lax
from jax.experimental import pallas as pl
from jax.experimental.pallas import tpu as pltpu
from jax.sharding import PartitionSpec as P

BF16, F32 = jnp.bfloat16, jnp.float32
MESH = pl.DeviceIdType.MESH
NZ, NX, NY, NS = 8, 2, 4, 4
LIMIT = 51
SPLIT = 2
WAVES, ROWS, LANES = 2 * SPLIT, 64 // SPLIT, 128
HALF = ROWS // 2
OWN = 16
AXES = (("y", "z"), ("z", "y")) * SPLIT
SIZE = {"y": NY, "z": NZ}
MESSAGES, LAST = 13, 5


def flip(value, bit):
    return value + bit - 2 * bit * lax.rem(lax.div(value, bit), 2)


RATE = {"x": 46.0e3, "y": 46.0e3, "z": 46.0e3, "core": 250.0e3, "xh": 46.0e3}
DELAY = {"x": 1.7, "y": 1.7, "z": 1.7, "core": 0.9, "xh": 2.5}
BLOCK = ROWS * LANES * 2


class Plan:
    def __init__(self):
        self.now, self.free, self.done = 0.0, {}, {}

    def spend(self, time):
        self.now += time

    def sent(self, link, way, size):
        begin = max(self.now, self.free.get((link, way), 0.0))
        self.free[link, way] = begin + size / RATE.get(link, 46.0e3)
        return self.free[link, way] + DELAY[link]

    def due(self, mark):
        return self.done.get(mark, float("inf")) if isinstance(mark, str) else mark

    def run(self, tasks):
        waiting = [[task, 0.0] for task in tasks]
        while waiting:
            entry = min(waiting, key=lambda pair: self.due(pair[1]))
            self.now = max(self.now, self.due(entry[1]))
            assert self.now < float("inf")
            value = next(entry[0], None)
            if value is None:
                waiting.remove(entry)
            elif isinstance(value, (str, float)):
                entry[1] = value
            else:
                waiting.append([value, 0.0])


def kernel(
    op_hbm, b_hbm, w_ref, d_ref, image0, image1, scalars,
    op, b_ref, spectra, part, part2, field0, field1, out, grad, core_in, x_in, xh_out, xh_in,
    w_all, ring_ya, ring_zb, ring_za, ring_yb, sums, sums_in,
    op_sem, b_sem, sens_s, sens_r, rs_s, rs_r, ag_s, ag_r, xh_s, xh_r, w_s, w_r, sum_s, sum_r,
):
    plan = Plan()
    s, q = lax.axis_index("sens"), lax.axis_index("src")
    z, xh, y = lax.div(q, 8), lax.rem(lax.div(q, 4), 2), lax.rem(q, 4)
    at = {"y": y, "z": z}
    rings = ((ring_ya, ring_zb), (ring_za, ring_yb))

    def device(s=s, z=z, xh=xh, y=y):
        return (s, z * 8 + xh * 4 + y)

    def along(axis, step):
        n = SIZE[axis]
        return device(**{axis: lax.rem(at[axis] + n + step, n)})

    core_peer, x_peer, xh_peer = device(s=flip(s, 1)), device(s=flip(s, 2)), device(xh=1 - xh)
    greeted = (
        core_peer, x_peer, xh_peer, *(along("y", d) for d in range(1, NY)),
        *(along("z", d) for d in range(1, NZ)),
    )

    def copy_of(src, dst, send_sem, recv_sem, to):
        return pltpu.make_async_remote_copy(
            src_ref=src, dst_ref=dst, send_sem=send_sem, recv_sem=recv_sem,
            device_id=to, device_id_type=MESH,
        )

    unsettled = {}

    def begin(name, copy, link, way, size):
        copy.start()
        unsettled.setdefault(name, []).append(copy)
        return plan.sent(link, way, size)

    def settle(name):
        for copy in unsettled.pop(name, ()):
            copy.wait_send()

    b_load = pltpu.make_async_copy(b_hbm, b_ref, b_sem)
    b_load.start()
    load = pltpu.make_async_copy(op_hbm, op, op_sem)
    load.start()
    barrier = pltpu.get_barrier_semaphore()
    for peer in greeted:
        pl.semaphore_signal(barrier, inc=1, device_id=peer, device_id_type=MESH)

    def rows(ref, i, wave):
        low = HALF * (wave // 2)
        parts = [ref[i, pl.ds(low, HALF)], ref[i, pl.ds(32 + low, HALF)]]
        return jnp.concatenate(parts, axis=0)

    def round_own(wave):
        def step(i, _):
            spectra[wave, s, i] = rows(b_ref, 2 * i + wave % 2, wave).astype(BF16)
            return 0
        lax.fori_loop(0, OWN, step, 0)

    b_load.wait()
    for wave in range(WAVES):
        round_own(wave)
    w_all[xh] = jnp.broadcast_to(w_ref[...][:, None, :], (2, 8, LANES))
    pl.semaphore_wait(barrier, len(greeted))

    def place(wave, zz, xx, yy):
        return yy * 16 + zz * 2 + xx if wave % 2 == 0 else zz * 8 + yy * 2 + xx

    def indices(block, i):
        return 2 * block + lax.div(i, 8), lax.rem(lax.div(i, 4), 2), lax.rem(i, 4)

    def forward(wave, one, two):
        def step(j, _):
            block, i = one + (two - one) * lax.div(j, OWN), lax.rem(j, OWN)
            zz, xx, yy = indices(block, i)
            out_ = lax.dot_general(
                spectra[wave, block, i], op[16 * zz + 8 * xx + 2 * yy + wave % 2],
                (((1,), (1,)), ((), ())), preferred_element_type=F32,
            )
            real = out_[:HALF, :LANES] - out_[HALF:, LANES:]
            imag = out_[HALF:, :LANES] + out_[:HALF, LANES:]
            part[wave, place(wave, zz, xx, yy)] = jnp.concatenate([real, imag], axis=0).astype(BF16)
            return 0
        lax.fori_loop(0, 2 * OWN, step, 0, unroll=16)
        plan.spend(1.4 / SPLIT + 0.2)

    def adjoint(wave, one, two):
        def step(j, _):
            block, i = one + (two - one) * lax.div(j, OWN), lax.rem(j, OWN)
            zz, xx, yy = indices(block, i)
            u = out[wave, place(wave, zz, xx, yy)]
            turned = jnp.concatenate([u[HALF:], -u[:HALF]], axis=0)
            f = 16 * zz + 8 * xx + 2 * yy + wave % 2
            g = jnp.dot(u, op[f, :LANES], preferred_element_type=F32)
            g += jnp.dot(turned, op[f, LANES:], preferred_element_type=F32)
            grad[wave, block, i] = g.astype(BF16)
            return 0
        lax.fori_loop(0, 2 * OWN, step, 0, unroll=16)
        plan.spend(1.4 / SPLIT + 0.2)

    def sens_begin(wave):
        mine, far = s, flip(s, 2)

        def move(k, block, to):
            ref = spectra.at[wave, block]
            return copy_of(ref, ref, sens_s.at[wave, k], sens_r.at[wave, k], to)

        size, name = OWN * BLOCK, ("spectra", wave)
        eta_x = begin(name, move(0, mine, x_peer), "x", 1, size)
        eta_core = begin(name, move(1, mine, core_peer), "core", 1, size)
        return eta_x, eta_core, move

    def sens_forward(wave, begun):
        mine, core, far, both = s, flip(s, 1), flip(s, 2), flip(flip(s, 1), 2)
        eta_x, eta_core, move = begun
        settle(("part", wave))
        settle(("out", wave))
        if not loaded:
            load.wait()
            loaded.append(True)
        yield eta_core
        move(1, core, core_peer).wait_recv()
        forward(wave, mine, core)
        yield eta_x
        move(0, far, x_peer).wait_recv()
        yield begin(("spectra", wave), move(2, far, core_peer), "core", 1, OWN * BLOCK)
        move(2, both, core_peer).wait_recv()
        forward(wave, far, both)

    def ring_sum(wave, level, ref, result, name):
        axis = AXES[wave][level]
        n, me = SIZE[axis], at[axis]
        piece = ref.shape[0] // n
        half, ring = piece // 2, rings[wave % 2][level].at[wave // 2]
        eta = {}

        top = n // 2

        def span(h):
            return (0, piece) if h is None else (h * half, half)

        def message(t, h, k):
            d = (1, -1)[k]
            dest = lax.rem(me + n + d * t, n)
            low, size = span(h)
            sems = (wave, level, k, t - 1, h or 0)
            return copy_of(
                ref.at[pl.ds(dest * piece + low, size)], ring.at[k, t - 1, pl.ds(low, size)],
                rs_s.at[sems], rs_r.at[sems], along(axis, d),
            )

        def go(t, h, k):
            eta[t, h, k] = begin(name, message(t, h, k), axis, k, span(h)[1] * BLOCK)

        def add(t, h, k):
            message(t, h, k).wait_recv()
            dest = lax.rem(me + n + (1, -1)[k] * (t - 1), n)
            low, size = span(h)

            def step(i, _):
                at_ = dest * piece + low + i
                total = ref[at_].astype(F32) + ring[k, t - 1, low + i].astype(F32)
                ref[at_] = total.astype(BF16)
                return 0
            lax.fori_loop(0, size, step, 0, unroll=min(size, 2))
            plan.spend(0.1 + 0.01 * size / SPLIT)

        for k in (0, 1):
            go(top, k, k)
        if level == 0:
            for k in (0, 1):
                go(top - 1, 1 - k, k)
        for t in range(top, 1, -1):
            whole = level == 1
            for k in (0, 1):
                h = k if t == top or not whole else None
                yield eta[t, h, k]
                add(t, h, k)
                go(t - 1, None if whole else k, k)
            if t - 1 > 1 and not whole:
                for k in (0, 1):
                    yield eta[t - 1, 1 - k, k]
                    add(t - 1, 1 - k, k)
                    go(t - 2, 1 - k, k)
        final = [(1, h, k) for h in ((None,) if level == 1 else (0, 1)) for k in (0, 1)]
        yield max(eta[key] for key in final)
        for key in final:
            message(*key).wait_recv()

        def last(i, _):
            total = ref[me * piece + i].astype(F32) + ring[0, 0, i].astype(F32)
            result(i, total + ring[1, 0, i].astype(F32))
            return 0
        lax.fori_loop(0, piece, last, 0, unroll=2)
        plan.spend(0.1 + 0.015 * piece / SPLIT)

    def ring_gather(wave, level, ref):
        axis = AXES[wave][level]
        n, me = SIZE[axis], at[axis]
        piece = ref.shape[0] // n
        half = piece // 2
        eta = {}
        top = n // 2

        def message(t, h, k, owner):
            low, size = (0, piece) if h is None else (h * half, half)
            sems = (wave, level, k, t - 1, h or 0)
            where = ref.at[pl.ds(owner * piece + low, size)]
            return copy_of(where, where, ag_s.at[sems], ag_r.at[sems], along(axis, (1, -1)[k]))

        def go(t, h, k):
            copy = message(t, h, k, lax.rem(me + n - (1, -1)[k] * (t - 1), n))
            size = (piece if h is None else half) * BLOCK
            eta[t, h, k] = begin(("out", wave), copy, axis, k, size)

        def got(t, h, k):
            message(t, h, k, lax.rem(me + n - (1, -1)[k] * t, n)).wait_recv()

        if level == 1:
            for k in (0, 1):
                go(1, None, k)
            for t in range(1, top):
                for k in (0, 1):
                    yield eta[t, None, k]
                    got(t, None, k)
                    go(t + 1, None if t + 1 < top else k, k)
        else:
            for first in (0, 1):
                for k in (0, 1):
                    go(1, k if first == 0 else 1 - k, k)
            for t in range(1, top):
                for k in (0, 1):
                    yield eta[t, k, k]
                    got(t, k, k)
                    go(t + 1, k, k)
                for k in (0, 1):
                    if t + 1 < top:
                        yield eta[t, 1 - k, k]
                        got(t, 1 - k, k)
                        go(t + 1, 1 - k, k)
        yield max(eta[top, k, k] for k in (0, 1))
        if level == 0:
            for k in (0, 1):
                got(top - 1, 1 - k, k)
        for k in (0, 1):
            got(top, k, k)

    def direct(wave, ref, sem, name, target, owner):
        axis = AXES[wave][1]
        n = SIZE[axis]
        piece = ref.shape[0] // n

        def message(d, owned):
            k, t = divmod(d - 1, n // 2)
            return copy_of(
                ref.at[pl.ds(owned * piece, piece)], target(k, t, owned * piece, piece),
                sem[0].at[wave, 1, k, t, 0], sem[1].at[wave, 1, k, t, 0], along(axis, d),
            )

        etas = []
        for d in sorted(range(1, n), key=lambda d: -min(d, n - d)):
            far = min(d, n - d)
            eta = begin(name, message(d, owner(d)), axis, int(2 * d > n), far * piece * BLOCK)
            etas.append(eta + 0.75 * (far - 1))
        return max(etas), message

    def direct_sum(wave, ref, result, name):
        axis = AXES[wave][1]
        n, me = SIZE[axis], at[axis]
        piece = ref.shape[0] // n
        ring = rings[wave % 2][1].at[wave // 2]

        def dest(d):
            return lax.rem(me + d, n)
        eta, message = direct(
            wave, ref, (rs_s, rs_r), name, lambda k, t, low, size: ring.at[k, t], dest
        )
        yield eta
        for d in range(1, n):
            message(d, dest(d)).wait_recv()
        for i in range(piece):
            total = ref[me * piece + i].astype(F32)
            for d in range(1, n):
                k, t = divmod(d - 1, n // 2)
                total += ring[k, t, i].astype(F32)
            result(i, total)
        plan.spend(0.3)

    def direct_gather(wave, ref):
        axis = AXES[wave][1]
        n, me = SIZE[axis], at[axis]
        eta, message = direct(
            wave, ref, (ag_s, ag_r), ("out", wave),
            lambda k, t, low, size: ref.at[pl.ds(low, size)], lambda d: me,
        )
        yield eta
        for d in range(1, n):
            message(d, lax.rem(me + n - d, n)).wait_recv()
        plan.spend(0.1)

    def reduce_field(wave, field):
        def keep2(i, total):
            part2[wave, i] = total.astype(BF16)

        def keep1(i, total):
            xh_out[wave, i] = total.astype(BF16)

        settle(("part2", wave))
        settle(("xh", wave))
        yield from ring_sum(wave, 0, part.at[wave], keep2, ("part", wave))
        share = part2.at[wave, pl.ds(0, 64 // SIZE[AXES[wave][0]])]
        yield from direct_sum(wave, share, keep1, ("part2", wave))
        copy = copy_of(xh_out.at[wave], xh_in.at[wave], xh_s.at[wave], xh_r.at[wave], xh_peer)
        yield begin(("xh", wave), copy, "xh", 1, 2 * BLOCK)
        copy.wait_recv()
        field[wave] = xh_out[wave].astype(F32) + xh_in[wave].astype(F32)

    def spread(wave):
        outer = AXES[wave][0]
        share = 64 // SIZE[outer]
        own = out.at[wave, pl.ds(at[outer] * share, share)]
        yield from direct_gather(wave, own)
        yield from ring_gather(wave, 0, out.at[wave])

    def sens_back(wave, image):
        mine, core, far, both = s, flip(s, 1), flip(s, 2), flip(flip(s, 1), 2)
        name, size = ("grad", wave), OWN * BLOCK

        def to_core(k, block):
            return copy_of(
                grad.at[wave, block], core_in.at[wave, k],
                sens_s.at[wave, 3 + k], sens_r.at[wave, 3 + k], core_peer,
            )

        settle(name)
        settle(("spectra", wave))
        adjoint(wave, both, far)
        first = to_core(0, both)
        eta = begin(name, first, "core", 1, size)
        yield eta
        first.wait_recv()

        def chip(i, _):
            total = grad[wave, far, i].astype(F32) + core_in[wave, 0, i].astype(F32)
            grad[wave, far, i] = total.astype(BF16)
            return 0
        lax.fori_loop(0, OWN, chip, 0, unroll=2)
        plan.spend(0.1 + 0.2 / SPLIT)
        across = copy_of(
            grad.at[wave, far], x_in.at[wave], sens_s.at[wave, 5], sens_r.at[wave, 5], x_peer
        )
        eta = begin(name, across, "x", 1, size)
        adjoint(wave, core, mine)
        second = to_core(1, core)
        begin(name, second, "core", 1, size)
        yield eta
        second.wait_recv()
        across.wait_recv()

        def whole(i, _):
            total = grad[wave, mine, i].astype(F32) + core_in[wave, 1, i].astype(F32)
            total += x_in[wave, i].astype(F32)
            at_ = 2 * i + wave % 2
            if image is image0:
                total += d_ref[at_] * rows(b_ref, at_, wave)
                spectra[wave, s, i] = total.astype(BF16)
            low = HALF * (wave // 2)
            image[at_, pl.ds(low, HALF)] = total[:HALF]
            image[at_, pl.ds(32 + low, HALF)] = total[HALF:]
            return 0
        lax.fori_loop(0, OWN, whole, 0, unroll=2)
        plan.spend(0.1 + 0.3 / SPLIT)

    def folded(value):
        return jnp.sum(value.reshape(-1, 8, LANES), axis=0)

    def total_of(turn):
        def message(m, source, to):
            return copy_of(
                source, sums_in.at[turn, m], sum_s.at[turn, m], sum_r.at[turn, m], to
            )

        for m, (link, peer) in enumerate((("core", core_peer), ("x", x_peer), ("xh", xh_peer))):
            copy = message(m, sums.at[turn, m], peer)
            yield begin("sums", copy, link, 1, 8192)
            copy.wait_recv()
            sums[turn, m + 1] = sums[turn, m] + sums_in[turn, m]
        m, level = 3, 3
        for axis in ("y", "z"):
            top = SIZE[axis] // 2
            total = sums[turn, level]
            last = [sums.at[turn, level]] * 2
            for t in range(1, top + 1):
                ways = (0, 1) if t < top else (0,)
                copies = []
                for k in ways:
                    copy = message(m, last[k], along(axis, (1, -1)[k]))
                    eta = begin("sums", copy, axis, k, 8192)
                    copies.append(copy)
                    last[k] = sums_in.at[turn, m]
                    m += 1
                yield eta
                for k in ways:
                    copies[k].wait_recv()
                    total = total + last[k][...]
            level += 1
            sums[turn, level] = total
        plan.done["total%d" % turn] = plan.now

    def scalar(turn, k):
        return jnp.sum(sums[turn, LAST, k], keepdims=True)

    loaded = []
    counts = {}
    zero = jnp.zeros((8, LANES), F32)

    def arrived(name):
        counts[name] = counts.get(name, 0) + 1
        if counts[name] == WAVES:
            plan.done[name] = plan.now

    def weigh(wave, field):
        for k in range(2):
            w = w_all[k, wave % 2, 0:1]
            u = w * field[wave, k]
            out[wave, place(wave, z, 0, y) + k] = u.astype(BF16)
        plan.spend(0.1 + 0.2 / SPLIT)

    def curve_of(first, second):
        total = zero
        for wave in range(WAVES):
            for k in range(2):
                y = field0[wave, k]
                if first is not None:
                    y = first * y - second * field1[wave, k]
                total += 0.5 * folded(w_all[k, wave % 2, 0:1] * y * y)
        return total

    def coefficients():
        rr0 = scalar(0, 0)
        return rr0 / scalar(0, 1), scalar(1, 0) / rr0

    def run(wave):
        yield from sens_forward(wave, begun[wave])
        yield from reduce_field(wave, field0)
        if "w" not in counts:
            w_copy.wait_recv()
            counts["w"] = 1
        weigh(wave, field0)
        arrived("weighed0")
        yield from spread(wave)
        yield from sens_back(wave, image0)
        now = sens_begin(wave)
        arrived("image")
        yield from sens_forward(wave, now)
        yield from reduce_field(wave, field1)
        weigh(wave, field1)
        arrived("weighed1")
        yield from spread(wave)
        yield from sens_back(wave, image1)

    def norms():
        yield "weighed0"
        sums[0, 0, 1] += curve_of(None, None)
        yield from total_of(0)
        yield "image"
        alpha = scalar(0, 0) / scalar(0, 1)

        def second(i, carry):
            residual = b_ref[i] - alpha * image0[i]
            return carry + folded(residual * residual)
        sums[1, 0, 0] = lax.fori_loop(0, 2 * OWN, second, zero)
        plan.spend(1.0)
        yield from total_of(1)
        yield "weighed1"
        alpha, beta = coefficients()

        def third(i, carry):
            p = (1.0 + beta) * b_ref[i] - alpha * image0[i]
            return carry + d_ref[i] * folded(p * p)
        sums[2, 0, 0] = curve_of(1.0 + beta, alpha) + lax.fori_loop(0, 2 * OWN, third, zero)
        plan.spend(1.0)
        yield from total_of(2)

    begun = [sens_begin(wave) for wave in range(WAVES)]
    w_copy = copy_of(w_all.at[xh], w_all.at[xh], w_s, w_r, xh_peer)
    begin("w", w_copy, "xh", 1, 8192)
    for turn in range(3):
        sums[turn, 0] = jnp.zeros((2, 8, LANES), F32)

    def first_norms(i, carry):
        square = folded(b_ref[i] * b_ref[i])
        return carry[0] + square, carry[1] + d_ref[i] * square
    rr, bdb = lax.fori_loop(0, 2 * OWN, first_norms, (zero, zero))
    sums[0, 0, 0] = rr
    sums[0, 0, 1] = bdb
    plan.spend(1.0)

    plan.run([*map(run, range(WAVES)), norms()])
    alpha, beta = coefficients()
    alpha1 = scalar(1, 0) / scalar(2, 0)
    for k, value in enumerate((alpha, beta, alpha1)):
        scalars[k] = jnp.broadcast_to(value, (8, LANES))
    for name in list(unsettled):
        settle(name)


def body(operator, right_side, noise_weights, damping):
    shape = right_side.shape
    op = operator.reshape(128, 256, LANES)
    b = right_side.reshape(2 * OWN, 2 * 32, LANES)
    block = (ROWS, LANES)
    vmem = pl.BlockSpec(memory_space=pltpu.VMEM)
    dma = pltpu.SemaphoreType.DMA
    scratch = [
        pltpu.VMEM((128, 256, LANES), BF16),
        pltpu.VMEM((2 * OWN, 2 * 32, LANES), F32),
        pltpu.VMEM((WAVES, NS, OWN, *block), BF16),
        pltpu.VMEM((WAVES, 64, *block), BF16),
        pltpu.VMEM((WAVES, 16, *block), BF16),
        pltpu.VMEM((WAVES, 2, *block), F32),
        pltpu.VMEM((WAVES, 2, *block), F32),
        pltpu.VMEM((WAVES, 64, *block), BF16),
        pltpu.VMEM((WAVES, NS, OWN, *block), BF16),
        pltpu.VMEM((WAVES, 2, OWN, *block), BF16),
        pltpu.VMEM((WAVES, OWN, *block), BF16),
        pltpu.VMEM((WAVES, 2, *block), BF16),
        pltpu.VMEM((WAVES, 2, *block), BF16),
        pltpu.VMEM((2, 2, 8, LANES), F32),
        pltpu.VMEM((SPLIT, 2, 2, 16, *block), BF16),
        pltpu.VMEM((SPLIT, 2, 4, 2, *block), BF16),
        pltpu.VMEM((SPLIT, 2, 4, 8, *block), BF16),
        pltpu.VMEM((SPLIT, 2, 2, 2, *block), BF16),
        pltpu.VMEM((3, LAST + 1, 2, 8, LANES), F32),
        pltpu.VMEM((3, MESSAGES, 2, 8, LANES), F32),
        dma, dma, dma((WAVES, 6)), dma((WAVES, 6)),
        dma((WAVES, 2, 2, 4, 2)), dma((WAVES, 2, 2, 4, 2)),
        dma((WAVES, 2, 2, 4, 2)), dma((WAVES, 2, 2, 4, 2)),
        dma((WAVES,)), dma((WAVES,)), dma, dma, dma((3, MESSAGES)), dma((3, MESSAGES)),
    ]
    result = jax.ShapeDtypeStruct(b.shape, F32)
    image0, image1, scalars = pl.pallas_call(
        kernel,
        out_shape=(result, result, jax.ShapeDtypeStruct((3, 8, LANES), F32)),
        in_specs=[
            pl.BlockSpec(memory_space=pltpu.HBM), pl.BlockSpec(memory_space=pltpu.HBM), vmem,
            pl.BlockSpec(memory_space=pltpu.SMEM),
        ],
        out_specs=(vmem, vmem, vmem),
        scratch_shapes=scratch,
        compiler_params=pltpu.CompilerParams(
            collective_id=0, has_side_effects=True, vmem_limit_bytes=LIMIT * 2**20
        ),
        name="solve",
    )(op, b, noise_weights, damping)
    alpha, beta, alpha1 = (scalars[k : k + 1, 0:1] for k in range(3))
    d = damping[:, None, None]
    residual = b - alpha * image0
    direction = residual + beta * b
    sol = alpha * b + alpha1 * direction
    res = residual - alpha1 * ((1.0 + beta) * image0 - alpha * (image1 + d * image0))
    return sol.reshape(shape), res.reshape(shape)


def solution(mesh):
    sides = P("sens", None, None, "src")
    return jax.shard_map(
        body,
        mesh=mesh,
        in_specs=(P(None, None, "sens", "src"), sides, P("src", "sens"), P("sens")),
        out_specs=(sides, sides),
        check_vma=False,
    )
```

```python
import functools

import jax
import jax.numpy as jnp
from jax import lax
from jax.experimental import pallas as pl
from jax.experimental.pallas import tpu as pltpu
from jax.sharding import PartitionSpec as P

BF16, F32 = jnp.bfloat16, jnp.float32
MESH = pl.DeviceIdType.MESH
NZ, NX, NY, NS = 8, 2, 4, 4
LIMIT = 51
SPLIT = 2
WAVES, ROWS, LANES = 2 * SPLIT, 64 // SPLIT, 128
HALF = ROWS // 2
OWN = 16
AXES = (("y", "z"), ("z", "y")) * SPLIT
SIZE = {"y": NY, "z": NZ}
MESSAGES, LAST = 13, 5


def flip(value, bit):
    return value + bit - 2 * bit * lax.rem(lax.div(value, bit), 2)


RATE = {"x": 46.0e3, "y": 46.0e3, "z": 46.0e3, "core": 250.0e3, "xh": 46.0e3}
DELAY = {"x": 1.7, "y": 1.7, "z": 1.7, "core": 0.9, "xh": 2.5}
BLOCK = ROWS * LANES * 2


class Plan:
    def __init__(self):
        self.now, self.free, self.done = 0.0, {}, {}

    def spend(self, time):
        self.now += time

    def sent(self, link, way, size):
        begin = max(self.now, self.free.get((link, way), 0.0))
        self.free[link, way] = begin + size / RATE.get(link, 46.0e3)
        return self.free[link, way] + DELAY[link]

    def due(self, mark):
        return self.done.get(mark, float("inf")) if isinstance(mark, str) else mark

    def run(self, tasks):
        waiting = [[task, 0.0] for task in tasks]
        while waiting:
            entry = min(waiting, key=lambda pair: self.due(pair[1]))
            self.now = max(self.now, self.due(entry[1]))
            assert self.now < float("inf")
            value = next(entry[0], None)
            if value is None:
                waiting.remove(entry)
            elif isinstance(value, (str, float)):
                entry[1] = value
            else:
                waiting.append([value, 0.0])


def kernel(
    op_hbm, b_hbm, w_ref, d_ref, image0, image1, scalars,
    op, b_ref, spectra, part, part2, field0, field1, out, grad, core_in, x_in, xh_out, xh_in,
    w_all, ring_ya, ring_zb, ring_za, ring_yb, sums, sums_in,
    op_sem, b_sem, sens_s, sens_r, rs_s, rs_r, ag_s, ag_r, xh_s, xh_r, w_s, w_r, sum_s, sum_r,
):
    plan = Plan()
    s, q = lax.axis_index("sens"), lax.axis_index("src")
    z, xh, y = lax.div(q, 8), lax.rem(lax.div(q, 4), 2), lax.rem(q, 4)
    at = {"y": y, "z": z}
    rings = ((ring_ya, ring_zb), (ring_za, ring_yb))

    def device(s=s, z=z, xh=xh, y=y):
        return (s, z * 8 + xh * 4 + y)

    def along(axis, step):
        n = SIZE[axis]
        return device(**{axis: lax.rem(at[axis] + n + step, n)})

    core_peer, x_peer, xh_peer = device(s=flip(s, 1)), device(s=flip(s, 2)), device(xh=1 - xh)
    greeted = (
        core_peer, x_peer, xh_peer, *(along("y", d) for d in range(1, NY)),
        *(along("z", d) for d in range(1, NZ)),
    )

    def copy_of(src, dst, send_sem, recv_sem, to):
        return pltpu.make_async_remote_copy(
            src_ref=src, dst_ref=dst, send_sem=send_sem, recv_sem=recv_sem,
            device_id=to, device_id_type=MESH,
        )

    unsettled = {}

    def begin(name, copy, link, way, size):
        copy.start()
        unsettled.setdefault(name, []).append(copy)
        return plan.sent(link, way, size)

    def settle(name):
        for copy in unsettled.pop(name, ()):
            copy.wait_send()

    b_load = pltpu.make_async_copy(b_hbm, b_ref, b_sem)
    b_load.start()
    load = pltpu.make_async_copy(op_hbm, op, op_sem)
    load.start()
    barrier = pltpu.get_barrier_semaphore()
    for peer in greeted:
        pl.semaphore_signal(barrier, inc=1, device_id=peer, device_id_type=MESH)

    def rows(ref, i, wave):
        low = HALF * (wave // 2)
        parts = [ref[i, pl.ds(low, HALF)], ref[i, pl.ds(32 + low, HALF)]]
        return jnp.concatenate(parts, axis=0)

    def round_own(wave):
        def step(i, _):
            spectra[wave, s, i] = rows(b_ref, 2 * i + wave % 2, wave).astype(BF16)
            return 0
        lax.fori_loop(0, OWN, step, 0)

    b_load.wait()
    for wave in range(WAVES):
        round_own(wave)
    w_all[xh] = jnp.broadcast_to(w_ref[...][:, None, :], (2, 8, LANES))
    pl.semaphore_wait(barrier, len(greeted))

    def place(wave, zz, xx, yy):
        return yy * 16 + zz * 2 + xx if wave % 2 == 0 else zz * 8 + yy * 2 + xx

    def indices(block, i):
        return 2 * block + lax.div(i, 8), lax.rem(lax.div(i, 4), 2), lax.rem(i, 4)

    def forward(wave, one, two):
        def step(j, _):
            block, i = one + (two - one) * lax.div(j, OWN), lax.rem(j, OWN)
            zz, xx, yy = indices(block, i)
            out_ = lax.dot_general(
                spectra[wave, block, i], op[16 * zz + 8 * xx + 2 * yy + wave % 2],
                (((1,), (1,)), ((), ())), preferred_element_type=F32,
            )
            real = out_[:HALF, :LANES] - out_[HALF:, LANES:]
            imag = out_[HALF:, :LANES] + out_[:HALF, LANES:]
            part[wave, place(wave, zz, xx, yy)] = jnp.concatenate([real, imag], axis=0).astype(BF16)
            return 0
        lax.fori_loop(0, 2 * OWN, step, 0, unroll=16)
        plan.spend(1.4 / SPLIT + 0.2)

    def adjoint(wave, one, two):
        def step(j, _):
            block, i = one + (two - one) * lax.div(j, OWN), lax.rem(j, OWN)
            zz, xx, yy = indices(block, i)
            u = out[wave, place(wave, zz, xx, yy)]
            turned = jnp.concatenate([u[HALF:], -u[:HALF]], axis=0)
            f = 16 * zz + 8 * xx + 2 * yy + wave % 2
            g = jnp.dot(u, op[f, :LANES], preferred_element_type=F32)
            g += jnp.dot(turned, op[f, LANES:], preferred_element_type=F32)
            grad[wave, block, i] = g.astype(BF16)
            return 0
        lax.fori_loop(0, 2 * OWN, step, 0, unroll=16)
        plan.spend(1.4 / SPLIT + 0.2)

    def sens_begin(wave):
        mine, far = s, flip(s, 2)

        def move(k, block, to):
            ref = spectra.at[wave, block]
            return copy_of(ref, ref, sens_s.at[wave, k], sens_r.at[wave, k], to)

        size, name = OWN * BLOCK, ("spectra", wave)
        eta_x = begin(name, move(0, mine, x_peer), "x", 1, size)
        eta_core = begin(name, move(1, mine, core_peer), "core", 1, size)
        return eta_x, eta_core, move

    def sens_forward(wave, begun):
        mine, core, far, both = s, flip(s, 1), flip(s, 2), flip(flip(s, 1), 2)
        eta_x, eta_core, move = begun
        settle(("part", wave))
        settle(("out", wave))
        if not loaded:
            load.wait()
            loaded.append(True)
        yield eta_core
        move(1, core, core_peer).wait_recv()
        forward(wave, mine, core)
        yield eta_x
        move(0, far, x_peer).wait_recv()
        yield begin(("spectra", wave), move(2, far, core_peer), "core", 1, OWN * BLOCK)
        move(2, both, core_peer).wait_recv()
        forward(wave, far, both)

    def ring_sum(wave, level, ref, result, name):
        axis = AXES[wave][level]
        n, me = SIZE[axis], at[axis]
        piece = ref.shape[0] // n
        half, ring = piece // 2, rings[wave % 2][level].at[wave // 2]
        eta = {}

        top = n // 2

        def span(h):
            return (0, piece) if h is None else (h * half, half)

        def message(t, h, k):
            d = (1, -1)[k]
            dest = lax.rem(me + n + d * t, n)
            low, size = span(h)
            sems = (wave, level, k, t - 1, h or 0)
            return copy_of(
                ref.at[pl.ds(dest * piece + low, size)], ring.at[k, t - 1, pl.ds(low, size)],
                rs_s.at[sems], rs_r.at[sems], along(axis, d),
            )

        def go(t, h, k):
            eta[t, h, k] = begin(name, message(t, h, k), axis, k, span(h)[1] * BLOCK)

        def add(t, h, k):
            message(t, h, k).wait_recv()
            dest = lax.rem(me + n + (1, -1)[k] * (t - 1), n)
            low, size = span(h)

            def step(i, _):
                at_ = dest * piece + low + i
                total = ref[at_].astype(F32) + ring[k, t - 1, low + i].astype(F32)
                ref[at_] = total.astype(BF16)
                return 0
            lax.fori_loop(0, size, step, 0, unroll=min(size, 2))
            plan.spend(0.1 + 0.01 * size / SPLIT)

        for k in (0, 1):
            go(top, k, k)
        if level == 0:
            for k in (0, 1):
                go(top - 1, 1 - k, k)
        for t in range(top, 1, -1):
            whole = level == 1
            for k in (0, 1):
                h = k if t == top or not whole else None
                yield eta[t, h, k]
                add(t, h, k)
                go(t - 1, None if whole else k, k)
            if t - 1 > 1 and not whole:
                for k in (0, 1):
                    yield eta[t - 1, 1 - k, k]
                    add(t - 1, 1 - k, k)
                    go(t - 2, 1 - k, k)
        final = [(1, h, k) for h in ((None,) if level == 1 else (0, 1)) for k in (0, 1)]
        yield max(eta[key] for key in final)
        for key in final:
            message(*key).wait_recv()

        def last(i, _):
            total = ref[me * piece + i].astype(F32) + ring[0, 0, i].astype(F32)
            result(i, total + ring[1, 0, i].astype(F32))
            return 0
        lax.fori_loop(0, piece, last, 0, unroll=2)
        plan.spend(0.1 + 0.015 * piece / SPLIT)

    def ring_gather(wave, level, ref):
        axis = AXES[wave][level]
        n, me = SIZE[axis], at[axis]
        piece = ref.shape[0] // n
        half = piece // 2
        eta = {}
        top = n // 2

        def message(t, h, k, owner):
            low, size = (0, piece) if h is None else (h * half, half)
            sems = (wave, level, k, t - 1, h or 0)
            where = ref.at[pl.ds(owner * piece + low, size)]
            return copy_of(where, where, ag_s.at[sems], ag_r.at[sems], along(axis, (1, -1)[k]))

        def go(t, h, k):
            copy = message(t, h, k, lax.rem(me + n - (1, -1)[k] * (t - 1), n))
            size = (piece if h is None else half) * BLOCK
            eta[t, h, k] = begin(("out", wave), copy, axis, k, size)

        def got(t, h, k):
            message(t, h, k, lax.rem(me + n - (1, -1)[k] * t, n)).wait_recv()

        if level == 1:
            for k in (0, 1):
                go(1, None, k)
            for t in range(1, top):
                for k in (0, 1):
                    yield eta[t, None, k]
                    got(t, None, k)
                    go(t + 1, None if t + 1 < top else k, k)
        else:
            for first in (0, 1):
                for k in (0, 1):
                    go(1, k if first == 0 else 1 - k, k)
            for t in range(1, top):
                for k in (0, 1):
                    yield eta[t, k, k]
                    got(t, k, k)
                    go(t + 1, k, k)
                for k in (0, 1):
                    if t + 1 < top:
                        yield eta[t, 1 - k, k]
                        got(t, 1 - k, k)
                        go(t + 1, 1 - k, k)
        yield max(eta[top, k, k] for k in (0, 1))
        if level == 0:
            for k in (0, 1):
                got(top - 1, 1 - k, k)
        for k in (0, 1):
            got(top, k, k)

    def direct(wave, ref, sem, name, target, owner):
        axis = AXES[wave][1]
        n = SIZE[axis]
        piece = ref.shape[0] // n

        def message(d, owned):
            k, t = divmod(d - 1, n // 2)
            return copy_of(
                ref.at[pl.ds(owned * piece, piece)], target(k, t, owned * piece, piece),
                sem[0].at[wave, 1, k, t, 0], sem[1].at[wave, 1, k, t, 0], along(axis, d),
            )

        etas = []
        for d in sorted(range(1, n), key=lambda d: -min(d, n - d)):
            far = min(d, n - d)
            eta = begin(name, message(d, owner(d)), axis, int(2 * d > n), far * piece * BLOCK)
            etas.append(eta + 0.75 * (far - 1))
        return max(etas), message

    def direct_sum(wave, ref, result, name):
        axis = AXES[wave][1]
        n, me = SIZE[axis], at[axis]
        piece = ref.shape[0] // n
        ring = rings[wave % 2][1].at[wave // 2]

        def dest(d):
            return lax.rem(me + d, n)
        eta, message = direct(
            wave, ref, (rs_s, rs_r), name, lambda k, t, low, size: ring.at[k, t], dest
        )
        yield eta
        for d in range(1, n):
            message(d, dest(d)).wait_recv()
        for i in range(piece):
            total = ref[me * piece + i].astype(F32)
            for d in range(1, n):
                k, t = divmod(d - 1, n // 2)
                total += ring[k, t, i].astype(F32)
            result(i, total)
        plan.spend(0.3)

    def direct_gather(wave, ref):
        axis = AXES[wave][1]
        n, me = SIZE[axis], at[axis]
        eta, message = direct(
            wave, ref, (ag_s, ag_r), ("out", wave),
            lambda k, t, low, size: ref.at[pl.ds(low, size)], lambda d: me,
        )
        yield eta
        for d in range(1, n):
            message(d, lax.rem(me + n - d, n)).wait_recv()
        plan.spend(0.1)

    def reduce_field(wave, field):
        def keep2(i, total):
            part2[wave, i] = total.astype(BF16)

        def keep1(i, total):
            xh_out[wave, i] = total.astype(BF16)

        settle(("part2", wave))
        settle(("xh", wave))
        yield from ring_sum(wave, 0, part.at[wave], keep2, ("part", wave))
        share = part2.at[wave, pl.ds(0, 64 // SIZE[AXES[wave][0]])]
        yield from direct_sum(wave, share, keep1, ("part2", wave))
        copy = copy_of(xh_out.at[wave], xh_in.at[wave], xh_s.at[wave], xh_r.at[wave], xh_peer)
        yield begin(("xh", wave), copy, "xh", 1, 2 * BLOCK)
        copy.wait_recv()
        field[wave] = xh_out[wave].astype(F32) + xh_in[wave].astype(F32)

    def spread(wave):
        outer = AXES[wave][0]
        share = 64 // SIZE[outer]
        own = out.at[wave, pl.ds(at[outer] * share, share)]
        yield from direct_gather(wave, own)
        yield from ring_gather(wave, 0, out.at[wave])

    def sens_back(wave, image):
        mine, core, far, both = s, flip(s, 1), flip(s, 2), flip(flip(s, 1), 2)
        name, size = ("grad", wave), OWN * BLOCK

        def to_core(k, block):
            return copy_of(
                grad.at[wave, block], core_in.at[wave, k],
                sens_s.at[wave, 3 + k], sens_r.at[wave, 3 + k], core_peer,
            )

        settle(name)
        settle(("spectra", wave))
        adjoint(wave, both, far)
        first = to_core(0, both)
        eta = begin(name, first, "core", 1, size)
        yield eta
        first.wait_recv()

        def chip(i, _):
            total = grad[wave, far, i].astype(F32) + core_in[wave, 0, i].astype(F32)
            grad[wave, far, i] = total.astype(BF16)
            return 0
        lax.fori_loop(0, OWN, chip, 0, unroll=2)
        plan.spend(0.1 + 0.2 / SPLIT)
        across = copy_of(
            grad.at[wave, far], x_in.at[wave], sens_s.at[wave, 5], sens_r.at[wave, 5], x_peer
        )
        eta = begin(name, across, "x", 1, size)
        adjoint(wave, core, mine)
        second = to_core(1, core)
        begin(name, second, "core", 1, size)
        yield eta
        second.wait_recv()
        across.wait_recv()

        def whole(i, _):
            total = grad[wave, mine, i].astype(F32) + core_in[wave, 1, i].astype(F32)
            total += x_in[wave, i].astype(F32)
            at_ = 2 * i + wave % 2
            if image is image0:
                total += d_ref[at_] * rows(b_ref, at_, wave)
                spectra[wave, s, i] = total.astype(BF16)
            low = HALF * (wave // 2)
            image[at_, pl.ds(low, HALF)] = total[:HALF]
            image[at_, pl.ds(32 + low, HALF)] = total[HALF:]
            return 0
        lax.fori_loop(0, OWN, whole, 0, unroll=2)
        plan.spend(0.1 + 0.3 / SPLIT)

    def folded(value):
        return jnp.sum(value.reshape(-1, 8, LANES), axis=0)

    def total_of(turn):
        def message(m, source, to):
            return copy_of(
                source, sums_in.at[turn, m], sum_s.at[turn, m], sum_r.at[turn, m], to
            )

        for m, (link, peer) in enumerate((("core", core_peer), ("x", x_peer), ("xh", xh_peer))):
            copy = message(m, sums.at[turn, m], peer)
            yield begin("sums", copy, link, 1, 8192)
            copy.wait_recv()
            sums[turn, m + 1] = sums[turn, m] + sums_in[turn, m]
        m, level = 3, 3
        for axis in ("y", "z"):
            top = SIZE[axis] // 2
            total = sums[turn, level]
            last = [sums.at[turn, level]] * 2
            for t in range(1, top + 1):
                ways = (0, 1) if t < top else (0,)
                copies = []
                for k in ways:
                    copy = message(m, last[k], along(axis, (1, -1)[k]))
                    eta = begin("sums", copy, axis, k, 8192)
                    copies.append(copy)
                    last[k] = sums_in.at[turn, m]
                    m += 1
                yield eta
                for k in ways:
                    copies[k].wait_recv()
                    total = total + last[k][...]
            level += 1
            sums[turn, level] = total
        plan.done["total%d" % turn] = plan.now

    def scalar(turn, k):
        return jnp.sum(sums[turn, LAST, k], keepdims=True)

    loaded = []
    counts = {}
    zero = jnp.zeros((8, LANES), F32)

    def arrived(name):
        counts[name] = counts.get(name, 0) + 1
        if counts[name] == WAVES:
            plan.done[name] = plan.now

    def weigh(wave, field):
        for k in range(2):
            w = w_all[k, wave % 2, 0:1]
            u = w * field[wave, k]
            out[wave, place(wave, z, 0, y) + k] = u.astype(BF16)
        plan.spend(0.1 + 0.2 / SPLIT)

    def curve_of(first, second):
        total = zero
        for wave in range(WAVES):
            for k in range(2):
                y = field0[wave, k]
                if first is not None:
                    y = first * y - second * field1[wave, k]
                total += 0.5 * folded(w_all[k, wave % 2, 0:1] * y * y)
        return total

    def coefficients():
        rr0 = scalar(0, 0)
        return rr0 / scalar(0, 1), scalar(1, 0) / rr0

    def run(wave):
        yield from sens_forward(wave, begun[wave])
        yield from reduce_field(wave, field0)
        if "w" not in counts:
            w_copy.wait_recv()
            counts["w"] = 1
        weigh(wave, field0)
        arrived("weighed0")
        yield from spread(wave)
        yield from sens_back(wave, image0)
        now = sens_begin(wave)
        arrived("image")
        yield from sens_forward(wave, now)
        yield from reduce_field(wave, field1)
        weigh(wave, field1)
        arrived("weighed1")
        yield from spread(wave)
        yield from sens_back(wave, image1)

    def norms():
        yield "weighed0"
        sums[0, 0, 1] += curve_of(None, None)
        yield from total_of(0)
        yield "image"
        alpha = scalar(0, 0) / scalar(0, 1)

        def second(i, carry):
            residual = b_ref[i] - alpha * image0[i]
            return carry + folded(residual * residual)
        sums[1, 0, 0] = lax.fori_loop(0, 2 * OWN, second, zero)
        plan.spend(1.0)
        yield from total_of(1)
        yield "weighed1"
        alpha, beta = coefficients()

        def third(i, carry):
            p = (1.0 + beta) * b_ref[i] - alpha * image0[i]
            return carry + d_ref[i] * folded(p * p)
        sums[2, 0, 0] = curve_of(1.0 + beta, alpha) + lax.fori_loop(0, 2 * OWN, third, zero)
        plan.spend(1.0)
        yield from total_of(2)

    begun = {wave: sens_begin(wave) for wave in (1, 0, 3, 2)}
    w_copy = copy_of(w_all.at[xh], w_all.at[xh], w_s, w_r, xh_peer)
    begin("w", w_copy, "xh", 1, 8192)
    for turn in range(3):
        sums[turn, 0] = jnp.zeros((2, 8, LANES), F32)

    def first_norms(i, carry):
        square = folded(b_ref[i] * b_ref[i])
        return carry[0] + square, carry[1] + d_ref[i] * square
    rr, bdb = lax.fori_loop(0, 2 * OWN, first_norms, (zero, zero))
    sums[0, 0, 0] = rr
    sums[0, 0, 1] = bdb
    plan.spend(1.0)

    plan.run([*map(run, range(WAVES)), norms()])
    alpha, beta = coefficients()
    alpha1 = scalar(1, 0) / scalar(2, 0)
    for k, value in enumerate((alpha, beta, alpha1)):
        scalars[k] = jnp.broadcast_to(value, (8, LANES))
    for name in list(unsettled):
        settle(name)


def body(operator, right_side, noise_weights, damping):
    shape = right_side.shape
    op = operator.reshape(128, 256, LANES)
    b = right_side.reshape(2 * OWN, 2 * 32, LANES)
    block = (ROWS, LANES)
    vmem = pl.BlockSpec(memory_space=pltpu.VMEM)
    dma = pltpu.SemaphoreType.DMA
    scratch = [
        pltpu.VMEM((128, 256, LANES), BF16),
        pltpu.VMEM((2 * OWN, 2 * 32, LANES), F32),
        pltpu.VMEM((WAVES, NS, OWN, *block), BF16),
        pltpu.VMEM((WAVES, 64, *block), BF16),
        pltpu.VMEM((WAVES, 16, *block), BF16),
        pltpu.VMEM((WAVES, 2, *block), F32),
        pltpu.VMEM((WAVES, 2, *block), F32),
        pltpu.VMEM((WAVES, 64, *block), BF16),
        pltpu.VMEM((WAVES, NS, OWN, *block), BF16),
        pltpu.VMEM((WAVES, 2, OWN, *block), BF16),
        pltpu.VMEM((WAVES, OWN, *block), BF16),
        pltpu.VMEM((WAVES, 2, *block), BF16),
        pltpu.VMEM((WAVES, 2, *block), BF16),
        pltpu.VMEM((2, 2, 8, LANES), F32),
        pltpu.VMEM((SPLIT, 2, 2, 16, *block), BF16),
        pltpu.VMEM((SPLIT, 2, 4, 2, *block), BF16),
        pltpu.VMEM((SPLIT, 2, 4, 8, *block), BF16),
        pltpu.VMEM((SPLIT, 2, 2, 2, *block), BF16),
        pltpu.VMEM((3, LAST + 1, 2, 8, LANES), F32),
        pltpu.VMEM((3, MESSAGES, 2, 8, LANES), F32),
        dma, dma, dma((WAVES, 6)), dma((WAVES, 6)),
        dma((WAVES, 2, 2, 4, 2)), dma((WAVES, 2, 2, 4, 2)),
        dma((WAVES, 2, 2, 4, 2)), dma((WAVES, 2, 2, 4, 2)),
        dma((WAVES,)), dma((WAVES,)), dma, dma, dma((3, MESSAGES)), dma((3, MESSAGES)),
    ]
    result = jax.ShapeDtypeStruct(b.shape, F32)
    image0, image1, scalars = pl.pallas_call(
        kernel,
        out_shape=(result, result, jax.ShapeDtypeStruct((3, 8, LANES), F32)),
        in_specs=[
            pl.BlockSpec(memory_space=pltpu.HBM), pl.BlockSpec(memory_space=pltpu.HBM), vmem,
            pl.BlockSpec(memory_space=pltpu.SMEM),
        ],
        out_specs=(vmem, vmem, vmem),
        scratch_shapes=scratch,
        compiler_params=pltpu.CompilerParams(
            collective_id=0, has_side_effects=True, vmem_limit_bytes=LIMIT * 2**20
        ),
        name="solve",
    )(op, b, noise_weights, damping)
    alpha, beta, alpha1 = (scalars[k : k + 1, 0:1] for k in range(3))
    d = damping[:, None, None]
    residual = b - alpha * image0
    direction = residual + beta * b
    sol = alpha * b + alpha1 * direction
    res = residual - alpha1 * ((1.0 + beta) * image0 - alpha * (image1 + d * image0))
    return sol.reshape(shape), res.reshape(shape)


def solution(mesh):
    sides = P("sens", None, None, "src")
    return jax.shard_map(
        body,
        mesh=mesh,
        in_specs=(P(None, None, "sens", "src"), sides, P("src", "sens"), P("sens")),
        out_specs=(sides, sides),
        check_vma=False,
    )
```
